256 devices in a mesh: section: 8 (over z), dp: 32 (over x, y, core).
Axes of the slice: x: 4, y: 4, z: 8, core: 2. Of those that a mesh axis runs over, the one named last changes fastest.
Arguments:
- inputs: bfloat16 [8192, 2048], P('dp'), may hold values from -6 to 6
- order: int32 [32, 2], P('dp'), may hold values from 0 to 1, each once within a row
- image_start: int32 [32, 2], P('dp'), may hold values from 0 to 112, as said below
- image_len: int32 [32, 2], P('dp'), may hold values from 16 to 64
- norm_gain: float32 [8, 2048], P('section'), may hold values from 0.25 to 1.75
- qkv_weight: bfloat16 [8, 2048, 6144], P('section', 'dp'), may hold values from -0.125 to 0.125
- q_gain: float32 [8, 2048], P('section'), may hold values from 0.5 to 2.5
- k_gain: float32 [8, 2048], P('section'), may hold values from 0.5 to 2.5
- o_weight: bfloat16 [8, 2048, 2048], P('section'), may hold values from -0.125 to 0.125
Outputs:
- section_outputs: bfloat16 [8, 8192, 2048], P('section', 'dp')
The draws below stay inside these ranges and needn't reach their ends.
Inputs may be any that keep to these rules, and one draw needn't show every extreme that they name: `order`: each row is a permutation of the micro-batch numbers. image_start + image_len <= 128 for every micro-batch.
All inputs are finite; a program needn't handle non-finite values.
Results may differ from the reference program's by a relative error of at most 0.035.
Values may be sent and summed in bfloat16 or wider, within the bound.
No kernel may reach another device: no remote copies, remote signals or barrier semaphores. Data moves between devices by JAX's collectives and lax.ppermute only.
A program may use at most 128 MiB of HBM per device.

```python
import math
import jax
import jax.numpy as jnp
from jax import lax

HEADS = 16
HEAD_DIM = 128
SEQ = 128
MICRO = 2
D = 2048
TOKENS = 8192
N_SECTION = 8
N_DP = 32


def span_pair(key):
    folded = jax.random.fold_in(key, 7)
    shortest = max(1, SEQ // 8)
    longest = SEQ // 2
    length = jax.random.randint(jax.random.fold_in(folded, 1), (N_DP, MICRO), shortest, longest + 1)
    random_bits = jax.random.randint(jax.random.fold_in(folded, 2), (N_DP, MICRO), 0, 1 << 20)
    chosen_group = jax.random.randint(jax.random.fold_in(folded, 3), (), 0, N_DP)
    chosen_micro = jax.random.randint(jax.random.fold_in(folded, 4), (), 0, MICRO)
    second_micro = (chosen_micro + 1) % MICRO
    group_index = jnp.arange(N_DP, dtype=jnp.int32)[:, None]
    micro_index = jnp.arange(MICRO, dtype=jnp.int32)[None, :]
    at_end = (group_index == chosen_group) & (micro_index == chosen_micro)
    at_long = (group_index == chosen_group) & (micro_index == second_micro)
    length = jnp.where(at_end, shortest, jnp.where(at_long, longest, length))
    start = random_bits % (SEQ - length + 1)
    start = jnp.where(at_end, SEQ - shortest, start)
    return (start.astype(jnp.int32), length.astype(jnp.int32))


def draw_image_start(key, part):
    return span_pair(key)[0]


def draw_image_len(key, part):
    return span_pair(key)[1]


def level_of(rng, shape, pieces, low, high):
    level, own = 1.0, jax.random.fold_in(rng, 6)
    for axis_at, shards_of in pieces:
        heights = jnp.exp(jax.random.uniform(jax.random.fold_in(own, axis_at), (shards_of,), jnp.float32, low / len(pieces), high / len(pieces)))
        level = level * jnp.repeat(heights, shape[axis_at] // shards_of).reshape([-1 if axis == axis_at else 1 for axis in range(len(shape))])
    return level


def scatter_about(stream_key, dims, deviation, most, cuts=(), kind=jnp.bfloat16):
    entries = deviation * jax.random.normal(stream_key, dims, jnp.float32)
    if cuts:
        entries = entries * level_of(stream_key, dims, cuts, -0.22, 0.18)
    return jnp.clip(entries, -most, most).astype(kind)


def setup_inputs(seed: int = 0) -> dict:
    keys = jax.random.split(jax.random.key(seed), 10)
    inputs = scatter_about(keys[0], (TOKENS, D), 1.0, 6.0, ((0, 32),))
    order = jax.vmap(lambda own: jax.random.permutation(own, MICRO))(jax.random.split(keys[1], N_DP)).reshape((N_DP, MICRO)).astype(jnp.int32)
    image_start = draw_image_start(jax.random.fold_in(keys[9], 71), 0)
    image_len = draw_image_len(jax.random.fold_in(keys[9], 71), 0)
    norm_gain = jnp.clip(1.0 + 0.15 * jax.random.normal(keys[4], (N_SECTION, D), jnp.float32), 0.25, 1.75)
    qkv_weight = scatter_about(keys[5], (N_SECTION, D, 3 * D), D ** -0.5, 0.125, ((0, 8), (1, 32)))
    q_gain = jnp.clip(jnp.exp(math.log(2.5) - 1.609438 * jax.random.uniform(keys[6], (N_SECTION, D), jnp.float32) ** level_of(keys[6], (N_SECTION, D), ((0, 8),), -0.2, 0.2)), 0.5, 2.5)
    k_gain = jnp.clip(jnp.exp(math.log(2.5) - 1.609438 * jax.random.uniform(keys[7], (N_SECTION, D), jnp.float32) ** level_of(keys[7], (N_SECTION, D), ((0, 8),), -0.2, 0.2)), 0.5, 2.5)
    o_weight = scatter_about(keys[8], (N_SECTION, D, D), D ** -0.5, 0.125, ((0, 8),))
    return dict(inputs=inputs, order=order, image_start=image_start, image_len=image_len, norm_gain=norm_gain, qkv_weight=qkv_weight, q_gain=q_gain, k_gain=k_gain, o_weight=o_weight)


epsilon_value = 1e-05

def normalize(hidden, gain):
    widened = hidden.astype(jnp.float32)
    mean_square = lax.optimization_barrier(jnp.mean(widened * widened, axis=-1, keepdims=True))
    return (widened * lax.rsqrt(mean_square + epsilon_value) * gain).astype(jnp.bfloat16)

def head_norm(block, gain, seq_len):
    split = block.reshape(seq_len, HEADS, HEAD_DIM)
    mean_square = lax.optimization_barrier(jnp.mean(split * split, axis=-1, keepdims=True))
    return (split * lax.rsqrt(mean_square + epsilon_value) * gain.reshape(HEADS, HEAD_DIM)).astype(jnp.bfloat16)

def finish(hidden, projected, gain_query, gain_key, out_weight, start, length):
    seq_len, model_width = hidden.shape
    queries = head_norm(projected[:, :model_width], gain_query, seq_len)
    key_rows = head_norm(projected[:, model_width:2 * model_width], gain_key, seq_len)
    value_rows = projected[:, 2 * model_width:].astype(jnp.bfloat16).reshape(seq_len, HEADS, HEAD_DIM)
    scores = jnp.einsum('qhd,khd->hqk', queries.astype(jnp.float32), key_rows.astype(jnp.float32)) * HEAD_DIM ** (-0.5)
    position = jnp.arange(seq_len, dtype=jnp.int32)
    in_image = (position >= start) & (position < start + length)
    allowed = (position[None, :] <= position[:, None]) | in_image[:, None] & in_image[None, :]
    scores = jnp.where(allowed[None], scores, -1e+30)
    row_max = lax.optimization_barrier(jnp.max(scores, axis=-1, keepdims=True))
    lifted = jnp.exp(scores - row_max)
    probabilities = (lifted / lax.optimization_barrier(jnp.sum(lifted, axis=-1, keepdims=True))).astype(jnp.bfloat16)
    mixed = jnp.einsum('hqk,khd->qhd', probabilities.astype(jnp.float32), value_rows.astype(jnp.float32))
    attended = mixed.reshape(seq_len, model_width).astype(jnp.bfloat16)
    output_rows = jnp.dot(attended, out_weight, preferred_element_type=jnp.float32)
    return (hidden.astype(jnp.float32) + output_rows).astype(jnp.bfloat16)

def reference(inputs, order, image_start, image_len, norm_gain, qkv_weight, q_gain, k_gain, o_weight):
    groups = inputs.reshape(N_DP, MICRO, SEQ, D)

    def one_group(packed):
        states, permutation, starts, lengths = packed
        states = states[permutation.astype(jnp.int32)]
        starts = starts[permutation.astype(jnp.int32)]
        lengths = lengths[permutation.astype(jnp.int32)]
        collected = []
        for section_number in range(N_SECTION):
            normed = normalize(states.reshape(MICRO * SEQ, D), norm_gain[section_number])
            projected = jnp.dot(normed, qkv_weight[section_number], preferred_element_type=jnp.float32)
            projected = projected.reshape(MICRO, SEQ, 3 * D)
            gain_query = q_gain[section_number]
            gain_key = k_gain[section_number]
            out_weight = o_weight[section_number]
            states = jax.vmap(lambda one, proj_rows, first, count: finish(one, proj_rows, gain_query, gain_key, out_weight, first, count))(states, projected, starts, lengths)
            collected.append(states)
        return jnp.stack(collected)
    result = lax.map(one_group, (groups, order, image_start, image_len))
    return jnp.transpose(result, (1, 0, 2, 3, 4)).reshape(N_SECTION, N_DP * MICRO * SEQ, D)
```

```python
import functools
import math

import jax
import jax.numpy as jnp
from jax import lax
from jax.experimental import pallas as pl
from jax.experimental.pallas import tpu as pltpu
from jax.sharding import PartitionSpec as P

HEADS = 16
HEAD_DIM = 128
GROUPS = 4
RESIDENT = 2
EPSILON = 1e-05
MIB = 1 << 20

ANY = pl.BlockSpec(memory_space=pl.ANY)
VMEM = pl.BlockSpec(memory_space=pltpu.VMEM)


def group_copies(w_hbm, target_of, sem_of, groups, width):
    model = w_hbm.shape[0]
    span = width // GROUPS
    copies = []
    for place, group in enumerate(groups):
        target = target_of(place)
        for part in range(3):
            copies.append(
                pltpu.make_async_copy(
                    w_hbm.at[:, pl.ds(part * width + group * span, span)],
                    target.at[:, pl.ds(part * span, span)],
                    sem_of(place, part),
                )
            )
    return copies


def load_body(w_hbm, o_hbm, w_keep, o_keep, w_sem, o_sem):
    model = o_hbm.shape[0]
    copies = group_copies(
        w_hbm, lambda place: w_keep.at[place], lambda place, part: w_sem.at[place, part],
        range(RESIDENT), model,
    )
    copies.append(pltpu.make_async_copy(o_hbm, o_keep, o_sem))
    for copy in copies:
        copy.start()
    for copy in copies:
        copy.wait()


def load_weights(qkv, out_weight):
    model = out_weight.shape[0]
    return pl.pallas_call(
        load_body,
        out_shape=(
            pltpu.VMEM((RESIDENT, model, 3 * model // GROUPS), qkv.dtype),
            pltpu.VMEM(out_weight.shape, out_weight.dtype),
        ),
        in_specs=[ANY, ANY],
        out_specs=[VMEM, VMEM],
        scratch_shapes=[pltpu.SemaphoreType.DMA((RESIDENT, 3)), pltpu.SemaphoreType.DMA],
        compiler_params=pltpu.CompilerParams(vmem_limit_bytes=1 * MIB),
        name="load_weights",
    )(qkv, out_weight)


def head_scale(block, ones):
    square = (block * block).astype(jnp.bfloat16)
    parts = []
    for at in range(0, block.shape[1], 2 * HEAD_DIM):
        parts.append(
            jnp.dot(
                square[:, at : at + 2 * HEAD_DIM], ones, preferred_element_type=jnp.float32
            )
        )
    total = jnp.concatenate(parts, axis=1)
    return lax.rsqrt(total * (1.0 / HEAD_DIM) + EPSILON)


def attend(projected, gain_query, gain_key, allowed, ones_pair, ones_column, span):
    query = projected[:, :span]
    key = projected[:, span : 2 * span]
    value = projected[:, 2 * span :].astype(jnp.bfloat16)
    query = (query * head_scale(query, ones_pair) * gain_query).astype(jnp.bfloat16)
    key = (key * head_scale(key, ones_pair) * gain_key).astype(jnp.bfloat16)
    heads = []
    for at in range(0, span, HEAD_DIM):
        cut = slice(at, at + HEAD_DIM)
        scores = lax.dot_general(
            query[:, cut], key[:, cut], (((1,), (1,)), ((), ())), preferred_element_type=jnp.float32
        )
        lifted = (jnp.exp2(scores) * allowed).astype(jnp.bfloat16)
        spread = jnp.concatenate([value[:, cut], ones_column], axis=1)
        mixed = jnp.dot(lifted, spread, preferred_element_type=jnp.float32)
        heads.append((mixed[:, :HEAD_DIM] / mixed[:, HEAD_DIM:]).astype(jnp.bfloat16))
    return heads


def turn_body(turn, last, micro, *refs):
    refs = list(refs)
    fresh_ref = refs.pop(0) if turn < micro else None
    hidden_ref = refs.pop(0) if turn > 0 else None
    before_ref = refs.pop(0) if turn > 0 else None
    if turn > 1:
        refs.pop(0)
    (allowed_ref, gain_ref, gain_query_ref, gain_key_ref, ones_ref, keep_ref, w_hbm, o_ref) = refs[:8]
    refs = refs[8:]
    after_ref = None if last else refs.pop(0)
    outputs = refs.pop(0) if turn > 0 else None
    state, normed, attended, stream, final, stream_sem, write_sem, final_sem = refs

    model = o_ref.shape[0]
    span = model // GROUPS
    section = lax.axis_index("section")
    slot = turn - section
    active = (slot >= 0) & (slot < micro)
    wrote = (slot >= 1) & (slot <= micro)

    if turn > 0:
        earlier = pltpu.make_async_copy(
            before_ref, outputs.at[jnp.clip(slot - 1, 0, micro - 1)], write_sem
        )

        @pl.when(wrote)
        def _():
            earlier.start()

    @pl.when(active)
    def _():
        streamed = group_copies(
            w_hbm, lambda place: stream.at[place], lambda place, part: stream_sem.at[place, part],
            range(RESIDENT, GROUPS), model,
        )
        for copy in streamed:
            copy.start()
        if turn == 0:
            state[...] = fresh_ref[0]
        elif turn < micro:

            @pl.when(section == 0)
            def _():
                state[...] = fresh_ref[turn]

            @pl.when(section != 0)
            def _():
                state[...] = hidden_ref[...]

        else:
            state[...] = hidden_ref[...]
        widened = state[...].astype(jnp.float32)
        mean_square = jnp.mean(widened * widened, axis=-1, keepdims=True)
        normed[...] = (widened * lax.rsqrt(mean_square + EPSILON) * gain_ref[...]).astype(
            jnp.bfloat16
        )
        allowed = allowed_ref[jnp.clip(slot, 0, micro - 1)]
        ones_pair = ones_ref[...]
        ones_column = jnp.ones((state.shape[0], HEAD_DIM), jnp.bfloat16)

        def project(group):
            if group < RESIDENT:
                weight = keep_ref.at[group]
            else:
                for copy in streamed[3 * (group - RESIDENT) : 3 * (group - RESIDENT) + 3]:
                    copy.wait()
                weight = stream.at[group - RESIDENT]
            return jnp.dot(normed[...], weight[...], preferred_element_type=jnp.float32)

        projected = project(0)
        for group in range(GROUPS):
            following = project(group + 1) if group + 1 < GROUPS else None
            cut = slice(group * span, (group + 1) * span)
            heads = attend(
                projected, gain_query_ref[:, cut], gain_key_ref[:, cut], allowed, ones_pair,
                ones_column, span,
            )
            for at, head in enumerate(heads):
                attended[:, group * span + at * HEAD_DIM : group * span + (at + 1) * HEAD_DIM] = head
            projected = following

        target = final if last else after_ref
        step = model // 4
        finals = []
        for at in range(0, model, step):
            cut = slice(at, at + step)
            product = jnp.dot(
                attended[...], o_ref[:, cut], preferred_element_type=jnp.float32
            )
            target[:, cut] = (state[:, cut].astype(jnp.float32) + product).astype(jnp.bfloat16)
            if last:
                copy = pltpu.make_async_copy(
                    final.at[:, cut],
                    outputs.at[jnp.clip(slot, 0, micro - 1), :, cut],
                    final_sem.at[at // step],
                )
                copy.start()
                finals.append(copy)
        for copy in finals:
            copy.wait()

    if turn > 0:

        @pl.when(wrote)
        def _():
            earlier.wait()


def take_turn(turn, last, micro, fresh, hidden, before, outputs, tables, keep, qkv, out_weight):
    rows, model = (fresh.shape[1], fresh.shape[2])
    operands, specs = [], []
    if turn < micro:
        operands.append(fresh)
        specs.append(VMEM)
    if turn > 0:
        operands += [hidden, before]
        specs += [VMEM, VMEM]
    aliases = {}
    if turn > 1:
        aliases = {len(operands): 0 if last else 1}
        operands.append(outputs)
        specs.append(ANY)
    operands += [*tables, keep, qkv, out_weight]
    specs += [VMEM] * len(tables) + [VMEM, ANY, VMEM]
    shapes, out_specs = [], []
    if not last:
        shapes.append(pltpu.VMEM((rows, model), jnp.bfloat16))
        out_specs.append(VMEM)
    if turn > 0:
        shapes.append(jax.ShapeDtypeStruct((micro, rows, model), jnp.bfloat16))
        out_specs.append(ANY)
    streams = GROUPS - RESIDENT
    results = pl.pallas_call(
        functools.partial(turn_body, turn, last, micro),
        out_shape=shapes,
        in_specs=specs,
        out_specs=out_specs,
        scratch_shapes=[
            pltpu.VMEM((rows, model), jnp.bfloat16),
            pltpu.VMEM((rows, model), jnp.bfloat16),
            pltpu.VMEM((rows, model), jnp.bfloat16),
            pltpu.VMEM((streams, model, 3 * model // GROUPS), jnp.bfloat16),
            pltpu.VMEM((rows, model) if last else (16, 128), jnp.bfloat16),
            pltpu.SemaphoreType.DMA((streams, 3)),
            pltpu.SemaphoreType.DMA,
            pltpu.SemaphoreType.DMA((4,)),
        ],
        input_output_aliases=aliases,
        compiler_params=pltpu.CompilerParams(vmem_limit_bytes=24 * MIB),
        name=f"turn_{turn}",
    )(*operands)
    after = None if last else results[0]
    outputs = results[-1] if turn > 0 else None
    return after, outputs


def body(inputs, order, image_start, image_len, norm_gain, qkv_weight, q_gain, k_gain, o_weight):
    section_count = lax.axis_size("section")
    micro = order.shape[1]
    row_count, model = inputs.shape
    rows = row_count // micro
    gathered = lax.all_gather(qkv_weight[0], "dp", axis=0, tiled=True)

    fresh = jnp.take(inputs.reshape(micro, rows, model), order[0], axis=0)
    starts = jnp.take(image_start[0], order[0])[:, None]
    ends = starts + jnp.take(image_len[0], order[0])[:, None]
    position = jnp.arange(rows, dtype=jnp.int32)
    inside = (position >= starts) & (position < ends)
    causal = position[None, :] <= position[:, None]
    allowed = (causal[None] | (inside[:, :, None] & inside[:, None, :])).astype(jnp.float32)
    gain_query = q_gain * (HEAD_DIM**-0.5 * math.log2(math.e))
    pair = jnp.arange(2 * HEAD_DIM, dtype=jnp.int32) // HEAD_DIM
    ones_pair = (pair[:, None] == pair[None, :]).astype(jnp.bfloat16)
    tables = (allowed, norm_gain, gain_query, k_gain, ones_pair)

    keep, out_weight = load_weights(gathered, o_weight[0])
    turns = micro + section_count - 1
    pairs = [(i, i + 1) for i in range(section_count - 1)]
    hidden = before = outputs = None
    for turn in range(turns):
        last = turn == turns - 1
        before, outputs = take_turn(
            turn, last, micro, fresh, hidden, before, outputs, tables, keep, gathered, out_weight
        )
        if not last:
            hidden = lax.ppermute(before, "section", pairs)
    return outputs.reshape(1, row_count, model)


def solution(mesh):
    in_specs = (
        P("dp", None),
        P("dp", None),
        P("dp", None),
        P("dp", None),
        P("section", None),
        P("section", "dp", None),
        P("section", None),
        P("section", None),
        P("section", None, None),
    )
    out_specs = P("section", "dp", None)
    return jax.shard_map(body, mesh=mesh, in_specs=in_specs, out_specs=out_specs, check_vma=False)
```

```python
import functools
import math

import jax
import jax.numpy as jnp
from jax import lax
from jax.experimental import pallas as pl
from jax.experimental.pallas import tpu as pltpu
from jax.sharding import PartitionSpec as P

HEADS = 16
HEAD_DIM = 128
GROUPS = 4
PARTS = 2
EPSILON = 1e-05
MIB = 1 << 20

HBM = pl.BlockSpec(memory_space=pltpu.HBM)
VMEM = pl.BlockSpec(memory_space=pltpu.VMEM)
SMEM = pl.BlockSpec(memory_space=pltpu.SMEM)


def group_copies(w_hbm, keep, sem, group, part):
    model = w_hbm.shape[0]
    span, depth = model // GROUPS, model // PARTS
    rows = pl.ds(part * depth, depth)
    return [
        pltpu.make_async_copy(
            w_hbm.at[rows, pl.ds(kind * model + group * span, span)],
            keep.at[group, rows, pl.ds(kind * span, span)],
            sem.at[group, kind],
        )
        for kind in range(3)
    ]


class Loads:
    def __init__(self, w_hbm, keep, sem, part):
        self.copies = [group_copies(w_hbm, keep, sem, group, part) for group in range(GROUPS)]

    def start(self, groups):
        for group in groups:
            for copy in self.copies[group]:
                copy.start()

    def wait(self, groups):
        for group in groups:
            for copy in self.copies[group]:
                copy.wait()

    def take(self, group):
        self.wait([group])
        if group + 2 < GROUPS:
            self.start([group + 2])

    def all(self):
        self.start(range(2, GROUPS))
        self.wait(range(GROUPS))


def load_body(o_hbm, o_keep, sem):
    copy = pltpu.make_async_copy(o_hbm, o_keep, sem)
    copy.start()
    copy.wait()


def load_out_weight(out_weight):
    return pl.pallas_call(
        load_body,
        out_shape=pltpu.VMEM(out_weight.shape, out_weight.dtype),
        in_specs=[HBM],
        out_specs=VMEM,
        scratch_shapes=[pltpu.SemaphoreType.DMA],
        compiler_params=pltpu.CompilerParams(vmem_limit_bytes=1 * MIB),
        name="load_out_weight",
    )(out_weight)


def position_of(turn, micro):
    section = lax.axis_index("section")
    slot = turn - section
    return section, slot, (slot >= 0) & (slot < micro)


def first_body(turn, micro, *refs):
    refs = list(refs)
    first_ref, inputs_ref, gains_ref, w_ref = refs[:4]
    refs = refs[4:]
    hidden_ref = refs.pop(0) if turn > 0 else None
    keep, partial_ref, state, load_sem, fresh_sem = refs
    keep = keep if turn == 0 else w_ref
    rows, depth = state.shape
    section, _, active = position_of(turn, micro)
    if turn < micro:
        fresh = pltpu.make_async_copy(
            inputs_ref.at[pl.ds(pl.multiple_of(first_ref[0, turn], rows), rows), pl.ds(0, depth)],
            state,
            fresh_sem,
        )
        pl.when(section == 0)(fresh.start)
    if turn == 0:
        loads = Loads(w_ref, keep, load_sem, 0)
        loads.start(range(2))
        pl.when(jnp.logical_not(active))(loads.all)

    @pl.when(active)
    def _():
        if turn == 0:
            fresh.wait()
        elif turn < micro:
            pl.when(section == 0)(fresh.wait)

            @pl.when(section != 0)
            def _():
                state[...] = hidden_ref[...]

        else:
            state[...] = hidden_ref[...]
        scaled = (state[...].astype(jnp.float32) * gains_ref[0:1, :depth]).astype(jnp.bfloat16)

        def multiply(group):
            partial_ref[group] = jnp.dot(
                scaled, keep[group, :depth, :], preferred_element_type=jnp.float32
            )

        if turn == 0:
            for group in range(GROUPS):
                loads.take(group)
                multiply(group)
        else:
            lax.fori_loop(0, GROUPS, lambda group, _: (multiply(group), 0)[1], 0)


def head_scale(block, ones, factor):
    square = (block * block).astype(jnp.bfloat16)
    parts = []
    for at in range(0, block.shape[1], 2 * HEAD_DIM):
        parts.append(
            jnp.dot(
                square[:, at : at + 2 * HEAD_DIM], ones, preferred_element_type=jnp.float32
            )
        )
    total = jnp.concatenate(parts, axis=1)
    return lax.rsqrt(total * (factor * factor * (1.0 / HEAD_DIM)) + EPSILON) * factor


def attend(projected, factor, gain_query, gain_key, allowed, ones_pair, ones_column, span):
    query = projected[:, :span]
    key = projected[:, span : 2 * span]
    value = (projected[:, 2 * span :] * factor).astype(jnp.bfloat16)
    query = (query * head_scale(query, ones_pair, factor) * gain_query).astype(jnp.bfloat16)
    key = (key * head_scale(key, ones_pair, factor) * gain_key).astype(jnp.bfloat16)
    heads = []
    for at in range(0, span, HEAD_DIM):
        cut = slice(at, at + HEAD_DIM)
        scores = lax.dot_general(
            query[:, cut], key[:, cut], (((1,), (1,)), ((), ())), preferred_element_type=jnp.float32
        )
        lifted = (jnp.exp2(scores) * allowed).astype(jnp.bfloat16)
        spread = jnp.concatenate([value[:, cut], ones_column], axis=1)
        mixed = jnp.dot(lifted, spread, preferred_element_type=jnp.float32)
        heads.append((mixed[:, :HEAD_DIM] / mixed[:, HEAD_DIM:]).astype(jnp.bfloat16))
    return heads


def second_body(turn, last, micro, *refs):
    refs = list(refs)
    first_ref, inputs_ref, allowed_ref, gains_ref, ones_ref, partial_ref, keep, o_ref = refs[:8]
    refs = refs[8:]
    w_ref = refs.pop(0) if turn == 0 else None
    hidden_refs, before_refs = (refs[:PARTS], refs[PARTS : 2 * PARTS]) if turn > 0 else ((), ())
    refs = refs[2 * PARTS :] if turn > 0 else refs
    if turn > 1:
        refs.pop(0)
    keep_out, _, *after_refs = refs[: 2 + PARTS]
    keep = keep_out if turn == 0 else keep
    refs = refs[2 + PARTS :]
    outputs = refs.pop(0) if turn > 0 else None
    state, scaled, attended, load_sem, fresh_sem, write_sem, final_sem = refs

    rows, model = state.shape
    span, depth = model // GROUPS, model // PARTS
    section, slot, active = position_of(turn, micro)
    wrote = (slot >= 1) & (slot <= micro)

    earlier = []
    if turn > 0:
        for part, before_ref in enumerate(before_refs):
            place = outputs.at[
                jnp.clip(slot - 1, 0, micro - 1), :, pl.ds(part * depth, depth)
            ]
            earlier.append(pltpu.make_async_copy(before_ref, place, write_sem.at[part]))

        @pl.when(wrote)
        def _():
            for copy in earlier:
                copy.start()

    if turn < micro:
        fresh = pltpu.make_async_copy(
            inputs_ref.at[pl.ds(pl.multiple_of(first_ref[0, turn], rows), rows)], state, fresh_sem
        )
        pl.when(section == 0)(fresh.start)
    if turn == 0:
        loads = Loads(w_ref, keep, load_sem, 1)
        loads.start(range(2))
        pl.when(jnp.logical_not(active))(loads.all)

    @pl.when(active)
    def _():
        def arrive():
            for part, hidden_ref in enumerate(hidden_refs):
                state[:, part * depth : (part + 1) * depth] = hidden_ref[...]

        if turn == 0:
            fresh.wait()
        elif turn < micro:
            pl.when(section == 0)(fresh.wait)
            pl.when(section != 0)(arrive)
        else:
            arrive()
        scaled[...] = (state[:, depth:].astype(jnp.float32) * gains_ref[0:1, depth:]).astype(
            jnp.bfloat16
        )
        widened = state[...].astype(jnp.float32)
        mean_square = jnp.mean(widened * widened, axis=-1, keepdims=True)
        factor = lax.rsqrt(mean_square + EPSILON)
        allowed = allowed_ref[jnp.clip(slot, 0, micro - 1)]
        ones_pair = ones_ref[...]
        ones_column = jnp.ones((rows, HEAD_DIM), jnp.bfloat16)

        def project(group):
            if turn == 0:
                loads.take(group)
            product = jnp.dot(
                scaled[...], keep[group, depth:, :], preferred_element_type=jnp.float32
            )
            return partial_ref[group] + product

        projected = project(0)
        for group in range(GROUPS):
            following = project(group + 1) if group + 1 < GROUPS else None
            cut = slice(group * span, (group + 1) * span)
            heads = attend(
                projected, factor, gains_ref[1:2, cut], gains_ref[2:3, cut], allowed, ones_pair,
                ones_column, span,
            )
            for at, head in enumerate(heads):
                attended[:, group * span + at * HEAD_DIM : group * span + (at + 1) * HEAD_DIM] = head
            projected = following

        finals = []
        for part, after_ref in enumerate(after_refs):
            cut = slice(part * depth, (part + 1) * depth)
            product = jnp.dot(attended[...], o_ref[:, cut], preferred_element_type=jnp.float32)
            after_ref[...] = (state[:, cut].astype(jnp.float32) + product).astype(jnp.bfloat16)
            if last:
                place = outputs.at[jnp.clip(slot, 0, micro - 1), :, pl.ds(part * depth, depth)]
                copy = pltpu.make_async_copy(after_ref, place, final_sem.at[part])
                copy.start()
                finals.append(copy)
        for copy in finals:
            copy.wait()

    if turn > 0:

        @pl.when(wrote)
        def _():
            for copy in earlier:
                copy.wait()


def keep_shapes(model):
    return (
        pltpu.VMEM((GROUPS, model, 3 * model // GROUPS), jnp.bfloat16),
        pltpu.VMEM((model, model), jnp.bfloat16),
    )


def first_half(turn, micro, rows, first, inputs, gains, weight, hidden):
    model = inputs.shape[1]
    depth = model // PARTS
    operands = [first, inputs, gains, weight] + ([hidden] if turn > 0 else [])
    return pl.pallas_call(
        functools.partial(first_body, turn, micro),
        out_shape=[
            keep_shapes(model)[0],
            pltpu.VMEM((GROUPS, rows, 3 * model // GROUPS), jnp.float32),
        ],
        in_specs=[SMEM, HBM, VMEM, VMEM if turn > 0 else HBM] + [VMEM] * (turn > 0),
        out_specs=[VMEM, VMEM],
        scratch_shapes=[
            pltpu.VMEM((rows, depth), jnp.bfloat16),
            pltpu.SemaphoreType.DMA((GROUPS, 3)),
            pltpu.SemaphoreType.DMA,
        ],
        input_output_aliases={3: 0} if turn > 0 else {},
        compiler_params=pltpu.CompilerParams(vmem_limit_bytes=8 * MIB),
        name=f"first_{turn}",
    )(*operands)


def second_half(turn, last, micro, rows, first, inputs, tables, partial, weights, qkv, hidden, before, outputs):
    model = inputs.shape[1]
    depth = model // PARTS
    operands = [first, inputs, *tables, partial, *weights]
    specs = [SMEM, HBM] + [VMEM] * (len(tables) + 3)
    aliases = {len(operands) - 2: 0, len(operands) - 1: 1}
    if turn == 0:
        operands.append(qkv)
        specs.append(HBM)
    else:
        operands += [*hidden, *before]
        specs += [VMEM] * 2 * PARTS
    if turn > 1:
        aliases[len(operands)] = 2 + PARTS
        operands.append(outputs)
        specs.append(HBM)
    shapes = [*keep_shapes(model)] + [pltpu.VMEM((rows, depth), jnp.bfloat16)] * PARTS
    out_specs = [VMEM] * (2 + PARTS)
    if turn > 0:
        shapes.append(pltpu.HBM((micro, rows, model), jnp.bfloat16))
        out_specs.append(HBM)
    results = pl.pallas_call(
        functools.partial(second_body, turn, last, micro),
        out_shape=shapes,
        in_specs=specs,
        out_specs=out_specs,
        scratch_shapes=[
            pltpu.VMEM((rows, model), jnp.bfloat16),
            pltpu.VMEM((rows, depth), jnp.bfloat16),
            pltpu.VMEM((rows, model), jnp.bfloat16),
            pltpu.SemaphoreType.DMA((GROUPS, 3)),
            pltpu.SemaphoreType.DMA,
            pltpu.SemaphoreType.DMA((PARTS,)),
            pltpu.SemaphoreType.DMA((PARTS,)),
        ],
        input_output_aliases=aliases,
        compiler_params=pltpu.CompilerParams(vmem_limit_bytes=8 * MIB),
        name=f"second_{turn}",
    )(*operands)
    return results[:2], results[2 : 2 + PARTS], results[2 + PARTS] if turn > 0 else None


def body(inputs, order, image_start, image_len, norm_gain, qkv_weight, q_gain, k_gain, o_weight):
    section_count = lax.axis_size("section")
    micro = order.shape[1]
    row_count, model = inputs.shape
    rows = row_count // micro
    gathered = lax.all_gather(qkv_weight[0], "dp", axis=0, tiled=True)

    starts = jnp.take(image_start[0], order[0])[:, None]
    ends = starts + jnp.take(image_len[0], order[0])[:, None]
    position = jnp.arange(rows, dtype=jnp.int32)
    inside = (position >= starts) & (position < ends)
    causal = position[None, :] <= position[:, None]
    allowed = (causal[None] | (inside[:, :, None] & inside[:, None, :])).astype(jnp.float32)
    gain_query = q_gain * (HEAD_DIM**-0.5 * math.log2(math.e))
    pair = jnp.arange(2 * HEAD_DIM, dtype=jnp.int32) // HEAD_DIM
    ones_pair = (pair[:, None] == pair[None, :]).astype(jnp.bfloat16)
    gains = jnp.concatenate([norm_gain, gain_query, k_gain], axis=0)
    tables = (allowed, gains, ones_pair)
    first = order * rows

    in_hbm = lambda array: pltpu.with_memory_space_constraint(array, pltpu.HBM)
    inputs = in_hbm(inputs)
    gathered = in_hbm(gathered)
    o_keep = load_out_weight(in_hbm(o_weight[0]))
    keep = gathered
    turns = micro + section_count - 1
    hidden = before = outputs = None
    for turn in range(turns):
        last = turn == turns - 1
        keep, partial = first_half(
            turn, micro, rows, first, inputs, gains, keep, hidden[0] if hidden else None
        )
        (keep, o_keep), before, outputs = second_half(
            turn, last, micro, rows, first, inputs, tables, partial, (keep, o_keep), gathered,
            hidden, before, outputs,
        )
        if not last:
            senders = range(max(0, turn - micro + 1), min(turn + 1, section_count - 1))
            pairs = [(i, i + 1) for i in senders]
            hidden = [lax.ppermute(part, "section", pairs) for part in before]
    return outputs.reshape(1, row_count, model)


def solution(mesh):
    in_specs = (
        P("dp", None),
        P("dp", None),
        P("dp", None),
        P("dp", None),
        P("section", None),
        P("section", "dp", None),
        P("section", None),
        P("section", None),
        P("section", None, None),
    )
    out_specs = P("section", "dp", None)
    return jax.shard_map(body, mesh=mesh, in_specs=in_specs, out_specs=out_specs, check_vma=False)
```

```python
import functools
import math

import jax
import jax.numpy as jnp
from jax import lax
from jax.experimental import pallas as pl
from jax.experimental.pallas import tpu as pltpu
from jax.sharding import PartitionSpec as P

HEADS = 16
HEAD_DIM = 128
GROUPS = 4
PARTS = 2
SINGLE = 5
EPSILON = 1e-05
MIB = 1 << 20

HBM = pl.BlockSpec(memory_space=pltpu.HBM)
VMEM = pl.BlockSpec(memory_space=pltpu.VMEM)
SMEM = pl.BlockSpec(memory_space=pltpu.SMEM)


class Loads:
    def __init__(self, w_hbm, o_hbm, keep, o_keep, sem):
        model = w_hbm.shape[0]
        span, half = model // GROUPS, model // 2
        self.stages = []
        for group in range(GROUPS):
            for rows in (pl.ds(0, half), pl.ds(half, half)):
                copies = []
                for kind in range(3):
                    copies.append(
                        pltpu.make_async_copy(
                            w_hbm.at[rows, pl.ds(kind * model + group * span, span)],
                            keep.at[group, rows, pl.ds(kind * span, span)],
                            sem.at[len(self.stages), kind],
                        )
                    )
                self.stages.append(copies)
        for rows in (pl.ds(0, half), pl.ds(half, half)):
            copy = pltpu.make_async_copy(
                o_hbm.at[rows], o_keep.at[rows], sem.at[len(self.stages), 0]
            )
            self.stages.append([copy])

    def start(self, stage):
        if stage < len(self.stages):
            for copy in self.stages[stage]:
                copy.start()

    def take(self, stages, flight=2):
        for stage in stages:
            for copy in self.stages[stage]:
                copy.wait()
            self.start(stage + flight)


def position_of(turn, micro):
    section = lax.axis_index("section")
    slot = turn - section
    return section, slot, (slot >= 0) & (slot < micro)


def first_body(turn, micro, *refs):
    if turn == 0:
        return
    first_ref, inputs_ref, gains_ref, keep, _, hidden_ref, _, _, partial_ref, state, fresh_sem = refs
    rows, depth = state.shape
    section, _, active = position_of(turn, micro)
    if turn < micro:
        fresh = pltpu.make_async_copy(
            inputs_ref.at[pl.ds(pl.multiple_of(first_ref[0, turn], rows), rows), pl.ds(0, depth)],
            state,
            fresh_sem,
        )
        pl.when(section == 0)(fresh.start)

    @pl.when(active)
    def _():
        if turn < micro:
            pl.when(section == 0)(fresh.wait)

            @pl.when(section != 0)
            def _():
                state[...] = hidden_ref[...]

        else:
            state[...] = hidden_ref[...]
        scaled = (state[...].astype(jnp.float32) * gains_ref[0:1, :depth]).astype(jnp.bfloat16)

        def multiply(group, _):
            partial_ref[group] = jnp.dot(
                scaled, keep[group, :depth, :], preferred_element_type=jnp.float32
            )
            return 0

        lax.fori_loop(0, GROUPS, multiply, 0)


def head_scale(block, ones, factor):
    square = (block * block).astype(jnp.bfloat16)
    parts = []
    for at in range(0, block.shape[1], 2 * HEAD_DIM):
        parts.append(
            jnp.dot(
                square[:, at : at + 2 * HEAD_DIM], ones, preferred_element_type=jnp.float32
            )
        )
    total = jnp.concatenate(parts, axis=1)
    return lax.rsqrt(total * (factor * factor * (1.0 / HEAD_DIM)) + EPSILON) * factor


def attend(projected, factor, gain_query, gain_key, allowed, ones_pair, ones_column, span):
    query = projected[:, :span]
    key = projected[:, span : 2 * span]
    value = (projected[:, 2 * span :] * factor).astype(jnp.bfloat16)
    query = (query * head_scale(query, ones_pair, factor) * gain_query).astype(jnp.bfloat16)
    key = (key * head_scale(key, ones_pair, factor) * gain_key).astype(jnp.bfloat16)
    heads = []
    for at in range(0, span, HEAD_DIM):
        cut = slice(at, at + HEAD_DIM)
        scores = lax.dot_general(
            query[:, cut], key[:, cut], (((1,), (1,)), ((), ())), preferred_element_type=jnp.float32
        )
        lifted = (jnp.exp2(scores) * allowed).astype(jnp.bfloat16)
        spread = jnp.concatenate([value[:, cut], ones_column], axis=1)
        mixed = jnp.dot(lifted, spread, preferred_element_type=jnp.float32)
        heads.append((mixed[:, :HEAD_DIM] / mixed[:, HEAD_DIM:]).astype(jnp.bfloat16))
    return heads


def second_body(turn, last, micro, *refs):
    refs = list(refs)
    first_ref, inputs_ref, allowed_ref, gains_ref, ones_ref, partial_ref, keep, o_ref = refs[:8]
    refs = refs[8:]
    w_hbm, o_hbm = (refs.pop(0), refs.pop(0)) if turn == 0 else (None, None)
    hidden_refs, before_refs = (refs[:PARTS], refs[PARTS : 2 * PARTS]) if turn > 0 else ((), ())
    refs = refs[2 * PARTS :] if turn > 0 else refs
    if turn > 1:
        refs.pop(0)
    keep_out, o_out, *after_refs = refs[: 2 + PARTS]
    keep, o_ref = (keep_out, o_out) if turn == 0 else (keep, o_ref)
    refs = refs[2 + PARTS :]
    outputs = refs.pop(0) if turn > 0 else None
    state, scaled, attended, fresh_sem, write_sem, final_sem, load_sem = refs

    rows, model = state.shape
    span, depth = model // GROUPS, model // PARTS
    begin = depth if turn > 0 else 0
    section, slot, active = position_of(turn, micro)
    wrote = (slot >= 1) & (slot <= micro)

    earlier = []
    if turn > 0:
        for part, before_ref in enumerate(before_refs):
            place = outputs.at[
                jnp.clip(slot - 1, 0, micro - 1), :, pl.ds(part * depth, depth)
            ]
            earlier.append(pltpu.make_async_copy(before_ref, place, write_sem.at[part]))

        @pl.when(wrote)
        def _():
            for copy in earlier:
                copy.start()

    if turn < micro:
        fresh = pltpu.make_async_copy(
            inputs_ref.at[pl.ds(pl.multiple_of(first_ref[0, turn], rows), rows)], state, fresh_sem
        )
        pl.when(section == 0)(fresh.start)
    if turn == 0:
        loads = Loads(w_hbm, o_hbm, keep, o_ref, load_sem)
        late = lax.rem(lax.axis_index("dp"), 2) == 1
        ahead = late | jnp.logical_not(active)
        everything = range(len(loads.stages))
        loads.start(0)

        @pl.when(jnp.logical_not(active & late))
        def _():
            loads.start(1)

        @pl.when(jnp.logical_not(active))
        def _():
            loads.take(everything)

        @pl.when(active & late)
        def _():
            loads.take(everything[:SINGLE], 1)
            loads.start(SINGLE + 1)
            loads.take(everything[SINGLE:])

    @pl.when(active)
    def _():
        def arrive():
            for part, hidden_ref in enumerate(hidden_refs):
                state[:, part * depth : (part + 1) * depth] = hidden_ref[...]

        if turn == 0:
            fresh.wait()
        elif turn < micro:
            pl.when(section == 0)(fresh.wait)
            pl.when(section != 0)(arrive)
        else:
            arrive()
        scaled[...] = (state[:, begin:].astype(jnp.float32) * gains_ref[0:1, begin:]).astype(
            jnp.bfloat16
        )
        widened = state[...].astype(jnp.float32)
        mean_square = jnp.mean(widened * widened, axis=-1, keepdims=True)
        factor = lax.rsqrt(mean_square + EPSILON)
        allowed = allowed_ref[jnp.clip(slot, 0, micro - 1)]
        ones_pair = ones_ref[...]
        ones_column = jnp.ones((rows, HEAD_DIM), jnp.bfloat16)

        def project(group):
            if turn == 0:
                stages = (2 * group, 2 * group + 1)
                pl.when(jnp.logical_not(ahead))(lambda: loads.take(stages))
            product = jnp.dot(
                scaled[...], keep[group, begin:, :], preferred_element_type=jnp.float32
            )
            return partial_ref[group] + product if turn > 0 else product

        projected = project(0)
        for group in range(GROUPS):
            following = project(group + 1) if group + 1 < GROUPS else None
            cut = slice(group * span, (group + 1) * span)
            heads = attend(
                projected, factor, gains_ref[1:2, cut], gains_ref[2:3, cut], allowed, ones_pair,
                ones_column, span,
            )
            for at, head in enumerate(heads):
                attended[:, group * span + at * HEAD_DIM : group * span + (at + 1) * HEAD_DIM] = head
            projected = following

        if turn == 0:
            pl.when(jnp.logical_not(ahead))(lambda: loads.take(everything[2 * GROUPS :]))
        finals = []
        for part, after_ref in enumerate(after_refs):
            width = model // 4

            def leave(at, _, part=part, after_ref=after_ref):
                here = pl.ds(pl.multiple_of(at * width, width), width)
                there = pl.ds(pl.multiple_of(part * depth + at * width, width), width)
                product = jnp.dot(
                    attended[...], o_ref[:, there], preferred_element_type=jnp.float32
                )
                after_ref[:, here] = (state[:, there].astype(jnp.float32) + product).astype(
                    jnp.bfloat16
                )
                return 0

            lax.fori_loop(0, depth // width, leave, 0)
            if last:
                place = outputs.at[jnp.clip(slot, 0, micro - 1), :, pl.ds(part * depth, depth)]
                copy = pltpu.make_async_copy(after_ref, place, final_sem.at[part])
                copy.start()
                finals.append(copy)
        for copy in finals:
            copy.wait()

    if turn > 0:

        @pl.when(wrote)
        def _():
            for copy in earlier:
                copy.wait()


def keep_shapes(model):
    return (
        pltpu.VMEM((GROUPS, model, 3 * model // GROUPS), jnp.bfloat16),
        pltpu.VMEM((model, model), jnp.bfloat16),
    )


def first_half(turn, micro, rows, first, inputs, gains, weights, hidden):
    model = inputs.shape[1]
    depth = model // PARTS
    operands = [first, inputs, gains, *weights] + ([hidden] if turn > 0 else [])
    return pl.pallas_call(
        functools.partial(first_body, turn, micro),
        out_shape=[
            *keep_shapes(model),
            pltpu.VMEM((GROUPS, rows, 3 * model // GROUPS), jnp.float32),
        ],
        in_specs=[SMEM, HBM, VMEM] + ([VMEM] * 3 if turn > 0 else [HBM]),
        out_specs=[VMEM, VMEM, VMEM],
        scratch_shapes=[
            pltpu.VMEM((rows, depth), jnp.bfloat16),
            pltpu.SemaphoreType.DMA,
        ],
        input_output_aliases={3: 0, 4: 1} if turn > 0 else {},
        compiler_params=pltpu.CompilerParams(vmem_limit_bytes=8 * MIB),
        name=f"first_{turn}",
    )(*operands)


def second_half(turn, last, micro, rows, first, inputs, tables, partial, weights, stored, hidden, before, outputs):
    model = inputs.shape[1]
    depth = model // PARTS
    operands = [first, inputs, *tables, partial, *weights]
    specs = [SMEM, HBM] + [VMEM] * (len(tables) + 3)
    aliases = {len(operands) - 2: 0, len(operands) - 1: 1}
    if turn == 0:
        operands += stored
        specs += [HBM, HBM]
    else:
        operands += [*hidden, *before]
        specs += [VMEM] * 2 * PARTS
    if turn > 1:
        aliases[len(operands)] = 2 + PARTS
        operands.append(outputs)
        specs.append(HBM)
    shapes = [*keep_shapes(model)] + [pltpu.VMEM((rows, depth), jnp.bfloat16)] * PARTS
    out_specs = [VMEM] * (2 + PARTS)
    if turn > 0:
        shapes.append(pltpu.HBM((micro, rows, model), jnp.bfloat16))
        out_specs.append(HBM)
    results = pl.pallas_call(
        functools.partial(second_body, turn, last, micro),
        out_shape=shapes,
        in_specs=specs,
        out_specs=out_specs,
        scratch_shapes=[
            pltpu.VMEM((rows, model), jnp.bfloat16),
            pltpu.VMEM((rows, depth if turn > 0 else model), jnp.bfloat16),
            pltpu.VMEM((rows, model), jnp.bfloat16),
            pltpu.SemaphoreType.DMA,
            pltpu.SemaphoreType.DMA((PARTS,)),
            pltpu.SemaphoreType.DMA((PARTS,)),
            pltpu.SemaphoreType.DMA((2 * GROUPS + 2, 3)),
        ],
        input_output_aliases=aliases,
        compiler_params=pltpu.CompilerParams(vmem_limit_bytes=8 * MIB),
        name=f"second_{turn}",
    )(*operands)
    return results[:2], results[2 : 2 + PARTS], results[2 + PARTS] if turn > 0 else None


def body(inputs, order, image_start, image_len, norm_gain, qkv_weight, q_gain, k_gain, o_weight):
    section_count = lax.axis_size("section")
    micro = order.shape[1]
    row_count, model = inputs.shape
    rows = row_count // micro
    gathered = lax.all_gather(qkv_weight[0], "dp", axis=0, tiled=True)

    starts = jnp.take(image_start[0], order[0])[:, None]
    ends = starts + jnp.take(image_len[0], order[0])[:, None]
    position = jnp.arange(rows, dtype=jnp.int32)
    inside = (position >= starts) & (position < ends)
    causal = position[None, :] <= position[:, None]
    allowed = (causal[None] | (inside[:, :, None] & inside[:, None, :])).astype(jnp.float32)
    gain_query = q_gain * (HEAD_DIM**-0.5 * math.log2(math.e))
    pair = jnp.arange(2 * HEAD_DIM, dtype=jnp.int32) // HEAD_DIM
    ones_pair = (pair[:, None] == pair[None, :]).astype(jnp.bfloat16)
    gains = jnp.concatenate([norm_gain, gain_query, k_gain], axis=0)
    tables = (allowed, gains, ones_pair)
    first = order * rows

    in_hbm = lambda array: pltpu.with_memory_space_constraint(array, pltpu.HBM)
    inputs = in_hbm(inputs)
    gathered = in_hbm(gathered)
    stored = (gathered, in_hbm(o_weight[0]))
    weights = stored[:1]
    turns = micro + section_count - 1
    hidden = before = outputs = None
    for turn in range(turns):
        last = turn == turns - 1
        *weights, partial = first_half(
            turn, micro, rows, first, inputs, gains, weights, hidden[0] if hidden else None
        )
        weights, before, outputs = second_half(
            turn, last, micro, rows, first, inputs, tables, partial, weights, stored,
            hidden, before, outputs,
        )
        if not last:
            senders = range(max(0, turn - micro + 1), min(turn + 1, section_count - 1))
            pairs = [(i, i + 1) for i in senders]
            hidden = [lax.ppermute(part, "section", pairs) for part in before]
    return outputs.reshape(1, row_count, model)


def solution(mesh):
    in_specs = (
        P("dp", None),
        P("dp", None),
        P("dp", None),
        P("dp", None),
        P("section", None),
        P("section", "dp", None),
        P("section", None),
        P("section", None),
        P("section", None, None),
    )
    out_specs = P("section", "dp", None)
    return jax.shard_map(body, mesh=mesh, in_specs=in_specs, out_specs=out_specs, check_vma=False)
```

```python
import functools
import math

import jax
import jax.numpy as jnp
from jax import lax
from jax.experimental import pallas as pl
from jax.experimental.pallas import tpu as pltpu
from jax.sharding import PartitionSpec as P

HEADS = 16
HEAD_DIM = 128
GROUPS = 4
PARTS = 2
SINGLE = 7
EPSILON = 1e-05
MIB = 1 << 20

HBM = pl.BlockSpec(memory_space=pltpu.HBM)
VMEM = pl.BlockSpec(memory_space=pltpu.VMEM)
SMEM = pl.BlockSpec(memory_space=pltpu.SMEM)


class Loads:
    def __init__(self, w_hbm, o_hbm, keep, o_keep, sem):
        model = w_hbm.shape[0]
        span, half = model // GROUPS, model // 2
        self.stages = []
        for group in range(GROUPS):
            for rows in (pl.ds(0, half), pl.ds(half, half)):
                copies = []
                for kind in range(3):
                    copies.append(
                        pltpu.make_async_copy(
                            w_hbm.at[rows, pl.ds(kind * model + group * span, span)],
                            keep.at[group, rows, pl.ds(kind * span, span)],
                            sem.at[len(self.stages), kind],
                        )
                    )
                self.stages.append(copies)
        for rows in (pl.ds(0, half), pl.ds(half, half)):
            copy = pltpu.make_async_copy(
                o_hbm.at[rows], o_keep.at[rows], sem.at[len(self.stages), 0]
            )
            self.stages.append([copy])

    def start(self, stage):
        if stage < len(self.stages):
            for copy in self.stages[stage]:
                copy.start()

    def take(self, stages, flight=2):
        for stage in stages:
            for copy in self.stages[stage]:
                copy.wait()
            self.start(stage + flight)


def position_of(turn, micro):
    section = lax.axis_index("section")
    slot = turn - section
    return section, slot, (slot >= 0) & (slot < micro)


def first_body(turn, micro, *refs):
    if turn == 0:
        return
    first_ref, inputs_ref, gains_ref, keep, _, hidden_ref, _, _, partial_ref, state, fresh_sem = refs
    rows, depth = state.shape
    section, _, active = position_of(turn, micro)
    if turn < micro:
        fresh = pltpu.make_async_copy(
            inputs_ref.at[pl.ds(pl.multiple_of(first_ref[0, turn], rows), rows), pl.ds(0, depth)],
            state,
            fresh_sem,
        )
        pl.when(section == 0)(fresh.start)

    @pl.when(active)
    def _():
        if turn < micro:
            pl.when(section == 0)(fresh.wait)

            @pl.when(section != 0)
            def _():
                state[...] = hidden_ref[...]

        else:
            state[...] = hidden_ref[...]
        scaled = (state[...].astype(jnp.float32) * gains_ref[0:1, :depth]).astype(jnp.bfloat16)

        def multiply(group, _):
            partial_ref[group] = jnp.dot(
                scaled, keep[group, :depth, :], preferred_element_type=jnp.float32
            )
            return 0

        lax.fori_loop(0, GROUPS, multiply, 0)


def head_scale(block, ones, factor):
    square = (block * block).astype(jnp.bfloat16)
    parts = []
    for at in range(0, block.shape[1], 2 * HEAD_DIM):
        parts.append(
            jnp.dot(
                square[:, at : at + 2 * HEAD_DIM], ones, preferred_element_type=jnp.float32
            )
        )
    total = jnp.concatenate(parts, axis=1)
    return lax.rsqrt(total * (factor * factor * (1.0 / HEAD_DIM)) + EPSILON) * factor


def attend(projected, factor, gain_query, gain_key, allowed, ones_pair, ones_column, span):
    query = projected[:, :span]
    key = projected[:, span : 2 * span]
    value = (projected[:, 2 * span :] * factor).astype(jnp.bfloat16)
    query = (query * head_scale(query, ones_pair, factor) * gain_query).astype(jnp.bfloat16)
    key = (key * head_scale(key, ones_pair, factor) * gain_key).astype(jnp.bfloat16)
    heads = []
    for at in range(0, span, HEAD_DIM):
        cut = slice(at, at + HEAD_DIM)
        scores = lax.dot_general(
            query[:, cut], key[:, cut], (((1,), (1,)), ((), ())), preferred_element_type=jnp.float32
        )
        lifted = (jnp.exp2(scores) * allowed).astype(jnp.bfloat16)
        spread = jnp.concatenate([value[:, cut], ones_column], axis=1)
        mixed = jnp.dot(lifted, spread, preferred_element_type=jnp.float32)
        heads.append((mixed[:, :HEAD_DIM] / mixed[:, HEAD_DIM:]).astype(jnp.bfloat16))
    return heads


def second_body(turn, last, micro, *refs):
    refs = list(refs)
    first_ref, inputs_ref, allowed_ref, gains_ref, ones_ref, partial_ref, keep, o_ref = refs[:8]
    refs = refs[8:]
    w_hbm, o_hbm = (refs.pop(0), refs.pop(0)) if turn == 0 else (None, None)
    hidden_refs, before_refs = (refs[:PARTS], refs[PARTS : 2 * PARTS]) if turn > 0 else ((), ())
    refs = refs[2 * PARTS :] if turn > 0 else refs
    if turn > 1:
        refs.pop(0)
    keep_out, o_out, *after_refs = refs[: 2 + PARTS]
    keep, o_ref = (keep_out, o_out) if turn == 0 else (keep, o_ref)
    refs = refs[2 + PARTS :]
    outputs = refs.pop(0) if turn > 0 else None
    state, scaled, attended, fresh_sem, write_sem, final_sem, load_sem = refs

    rows, model = state.shape
    span, depth = model // GROUPS, model // PARTS
    begin = depth if turn > 0 else 0
    section, slot, active = position_of(turn, micro)
    wrote = (slot >= 1) & (slot <= micro)

    earlier = []
    if turn > 0:
        for part, before_ref in enumerate(before_refs):
            place = outputs.at[
                jnp.clip(slot - 1, 0, micro - 1), :, pl.ds(part * depth, depth)
            ]
            earlier.append(pltpu.make_async_copy(before_ref, place, write_sem.at[part]))

        @pl.when(wrote)
        def _():
            for copy in earlier:
                copy.start()

    if turn < micro:
        fresh = pltpu.make_async_copy(
            inputs_ref.at[pl.ds(pl.multiple_of(first_ref[0, turn], rows), rows)], state, fresh_sem
        )
        pl.when(section == 0)(fresh.start)
    if turn == 0:
        loads = Loads(w_hbm, o_hbm, keep, o_ref, load_sem)
        late = lax.rem(lax.axis_index("dp"), 2) == 1
        ahead = late | jnp.logical_not(active)
        everything = range(len(loads.stages))
        loads.start(0)

        @pl.when(jnp.logical_not(active & late))
        def _():
            loads.start(1)

        @pl.when(jnp.logical_not(active))
        def _():
            loads.take(everything)

        @pl.when(active & late)
        def _():
            loads.take(everything[:SINGLE], 1)
            loads.start(SINGLE + 1)
            loads.take(everything[SINGLE:])

    @pl.when(active)
    def _():
        def arrive():
            for part, hidden_ref in enumerate(hidden_refs):
                state[:, part * depth : (part + 1) * depth] = hidden_ref[...]

        if turn == 0:
            fresh.wait()
        elif turn < micro:
            pl.when(section == 0)(fresh.wait)
            pl.when(section != 0)(arrive)
        else:
            arrive()
        scaled[...] = (state[:, begin:].astype(jnp.float32) * gains_ref[0:1, begin:]).astype(
            jnp.bfloat16
        )
        widened = state[...].astype(jnp.float32)
        mean_square = jnp.mean(widened * widened, axis=-1, keepdims=True)
        factor = lax.rsqrt(mean_square + EPSILON)
        allowed = allowed_ref[jnp.clip(slot, 0, micro - 1)]
        ones_pair = ones_ref[...]
        ones_column = jnp.ones((rows, HEAD_DIM), jnp.bfloat16)

        def project(group):
            if turn == 0:
                stages = (2 * group, 2 * group + 1)
                pl.when(jnp.logical_not(ahead))(lambda: loads.take(stages))
            product = jnp.dot(
                scaled[...], keep[group, begin:, :], preferred_element_type=jnp.float32
            )
            return partial_ref[group] + product if turn > 0 else product

        projected = project(0)
        for group in range(GROUPS):
            following = project(group + 1) if group + 1 < GROUPS else None
            cut = slice(group * span, (group + 1) * span)
            heads = attend(
                projected, factor, gains_ref[1:2, cut], gains_ref[2:3, cut], allowed, ones_pair,
                ones_column, span,
            )
            for at, head in enumerate(heads):
                attended[:, group * span + at * HEAD_DIM : group * span + (at + 1) * HEAD_DIM] = head
            projected = following

        if turn == 0:
            pl.when(jnp.logical_not(ahead))(lambda: loads.take(everything[2 * GROUPS :]))
        finals = []
        for part, after_ref in enumerate(after_refs):
            width = model // 4

            def leave(at, _, part=part, after_ref=after_ref):
                here = pl.ds(pl.multiple_of(at * width, width), width)
                there = pl.ds(pl.multiple_of(part * depth + at * width, width), width)
                product = jnp.dot(
                    attended[...], o_ref[:, there], preferred_element_type=jnp.float32
                )
                after_ref[:, here] = (state[:, there].astype(jnp.float32) + product).astype(
                    jnp.bfloat16
                )
                return 0

            if not last:
                lax.fori_loop(0, depth // width, leave, 0)
                continue
            for at in range(depth // width):
                leave(at, 0)
                columns = pl.ds(part * depth + at * width, width)
                copy = pltpu.make_async_copy(
                    after_ref.at[:, pl.ds(at * width, width)],
                    outputs.at[jnp.clip(slot, 0, micro - 1), :, columns],
                    final_sem.at[part, at],
                )
                copy.start()
                finals.append(copy)
        for copy in finals:
            copy.wait()

    if turn > 0:

        @pl.when(wrote)
        def _():
            for copy in earlier:
                copy.wait()


def keep_shapes(model):
    return (
        pltpu.VMEM((GROUPS, model, 3 * model // GROUPS), jnp.bfloat16),
        pltpu.VMEM((model, model), jnp.bfloat16),
    )


def first_half(turn, micro, rows, first, inputs, gains, weights, hidden):
    model = inputs.shape[1]
    depth = model // PARTS
    operands = [first, inputs, gains, *weights] + ([hidden] if turn > 0 else [])
    return pl.pallas_call(
        functools.partial(first_body, turn, micro),
        out_shape=[
            *keep_shapes(model),
            pltpu.VMEM((GROUPS, rows, 3 * model // GROUPS), jnp.float32),
        ],
        in_specs=[SMEM, HBM, VMEM] + ([VMEM] * 3 if turn > 0 else [HBM]),
        out_specs=[VMEM, VMEM, VMEM],
        scratch_shapes=[
            pltpu.VMEM((rows, depth), jnp.bfloat16),
            pltpu.SemaphoreType.DMA,
        ],
        input_output_aliases={3: 0, 4: 1} if turn > 0 else {},
        compiler_params=pltpu.CompilerParams(vmem_limit_bytes=8 * MIB),
        name=f"first_{turn}",
    )(*operands)


def second_half(turn, last, micro, rows, first, inputs, tables, partial, weights, stored, hidden, before, outputs):
    model = inputs.shape[1]
    depth = model // PARTS
    operands = [first, inputs, *tables, partial, *weights]
    specs = [SMEM, HBM] + [VMEM] * (len(tables) + 3)
    aliases = {len(operands) - 2: 0, len(operands) - 1: 1}
    if turn == 0:
        operands += stored
        specs += [HBM, HBM]
    else:
        operands += [*hidden, *before]
        specs += [VMEM] * 2 * PARTS
    if turn > 1:
        aliases[len(operands)] = 2 + PARTS
        operands.append(outputs)
        specs.append(HBM)
    shapes = [*keep_shapes(model)] + [pltpu.VMEM((rows, depth), jnp.bfloat16)] * PARTS
    out_specs = [VMEM] * (2 + PARTS)
    if turn > 0:
        shapes.append(pltpu.HBM((micro, rows, model), jnp.bfloat16))
        out_specs.append(HBM)
    results = pl.pallas_call(
        functools.partial(second_body, turn, last, micro),
        out_shape=shapes,
        in_specs=specs,
        out_specs=out_specs,
        scratch_shapes=[
            pltpu.VMEM((rows, model), jnp.bfloat16),
            pltpu.VMEM((rows, depth if turn > 0 else model), jnp.bfloat16),
            pltpu.VMEM((rows, model), jnp.bfloat16),
            pltpu.SemaphoreType.DMA,
            pltpu.SemaphoreType.DMA((PARTS,)),
            pltpu.SemaphoreType.DMA((PARTS, 4 // PARTS)),
            pltpu.SemaphoreType.DMA((2 * GROUPS + 2, 3)),
        ],
        input_output_aliases=aliases,
        compiler_params=pltpu.CompilerParams(vmem_limit_bytes=8 * MIB),
        name=f"second_{turn}",
    )(*operands)
    return results[:2], results[2 : 2 + PARTS], results[2 + PARTS] if turn > 0 else None


def body(inputs, order, image_start, image_len, norm_gain, qkv_weight, q_gain, k_gain, o_weight):
    section_count = lax.axis_size("section")
    micro = order.shape[1]
    row_count, model = inputs.shape
    rows = row_count // micro
    gathered = lax.all_gather(qkv_weight[0], "dp", axis=0, tiled=True)

    starts = jnp.take(image_start[0], order[0])[:, None]
    ends = starts + jnp.take(image_len[0], order[0])[:, None]
    position = jnp.arange(rows, dtype=jnp.int32)
    inside = (position >= starts) & (position < ends)
    causal = position[None, :] <= position[:, None]
    allowed = (causal[None] | (inside[:, :, None] & inside[:, None, :])).astype(jnp.float32)
    gain_query = q_gain * (HEAD_DIM**-0.5 * math.log2(math.e))
    pair = jnp.arange(2 * HEAD_DIM, dtype=jnp.int32) // HEAD_DIM
    ones_pair = (pair[:, None] == pair[None, :]).astype(jnp.bfloat16)
    gains = jnp.concatenate([norm_gain, gain_query, k_gain], axis=0)
    tables = (allowed, gains, ones_pair)
    first = order * rows

    in_hbm = lambda array: pltpu.with_memory_space_constraint(array, pltpu.HBM)
    inputs = in_hbm(inputs)
    gathered = in_hbm(gathered)
    stored = (gathered, in_hbm(o_weight[0]))
    weights = stored[:1]
    turns = micro + section_count - 1
    hidden = before = outputs = None
    for turn in range(turns):
        last = turn == turns - 1
        *weights, partial = first_half(
            turn, micro, rows, first, inputs, gains, weights, hidden[0] if hidden else None
        )
        weights, before, outputs = second_half(
            turn, last, micro, rows, first, inputs, tables, partial, weights, stored,
            hidden, before, outputs,
        )
        if not last:
            senders = range(max(0, turn - micro + 1), min(turn + 1, section_count - 1))
            pairs = [(i, i + 1) for i in senders]
            hidden = [lax.ppermute(part, "section", pairs) for part in before]
    return outputs.reshape(1, row_count, model)


def solution(mesh):
    in_specs = (
        P("dp", None),
        P("dp", None),
        P("dp", None),
        P("dp", None),
        P("section", None),
        P("section", "dp", None),
        P("section", None),
        P("section", None),
        P("section", None, None),
    )
    out_specs = P("section", "dp", None)
    return jax.shard_map(body, mesh=mesh, in_specs=in_specs, out_specs=out_specs, check_vma=False)
```
